128 devices in a mesh: pb: 16 (over z, x_lo, core), pa: 8 (over y, x_hi).
Axes of the slice: x: 4 (x_hi: 2, x_lo: 2; x = x_hi * 2 + x_lo), y: 4, z: 4, core: 2. Of those that a mesh axis runs over, the one named last changes fastest.
Arguments:
- queries: float32 [16384, 1024], P('pb'), may hold values from -64 to 64
- passages: float32 [16384, 1024], P(('pb', 'pa')), may hold values from -64 to 64
- hard_ids: int32 [16384, 7], P('pb'), may hold values from 0 to 16383
Outputs:
- loss: float32 [], replicated
- query_grads: float32 [16384, 1024], P(('pb', 'pa'))
- passage_grads: float32 [16384, 1024], P(('pb', 'pa'))
The draws below stay inside these ranges and needn't reach their ends.
All inputs are finite; a program needn't handle non-finite values.
Results may differ from the reference program's by a relative error of at most 0.0003.
Values sent between devices are 32-bit elements; how exact they have to be, the bound alone decides.
No kernel may reach another device: no remote copies, remote signals or barrier semaphores. Data moves between devices by JAX's collectives and lax.ppermute only.
A program may use at most 128 MiB of HBM per device.

```python
import math
import jax
import jax.numpy as jnp
import numpy as np
from jax import lax

D = 1024
HARD = 7
NQ = 16384
NP = 16384


def joint_embeddings(key):
    query_base = jnp.clip(jax.random.normal(jax.random.fold_in(key, 11), (NQ, D), jnp.float32), -6.0, 6.0)
    passage_base = jnp.clip(jax.random.normal(jax.random.fold_in(key, 12), (NP, D), jnp.float32), -6.0, 6.0)
    noise = jnp.clip(jax.random.normal(jax.random.fold_in(key, 13), (NP, D), jnp.float32), -6.0, 6.0)
    rows = jnp.arange(NP, dtype=jnp.int32)[:, None]
    strength = 160.0 + 20.0 * (rows // 16 % 5).astype(jnp.float32)
    amplitude = strength / (0.8 * math.sqrt(D))
    partner = rows % 16 == 4
    shifted = jnp.roll(passage_base, 1, axis=0) + 2.0 / amplitude * noise
    passage_base = jnp.where(partner, shifted, passage_base)
    qrows = jnp.arange(NQ, dtype=jnp.int32)[:, None]
    chosen = qrows % 16 == 3
    query_base = jnp.where(chosen, amplitude * jnp.sign(passage_base), query_base)
    return (query_base, passage_base)


def draw_queries(key, part):
    return joint_embeddings(key)[0]


def draw_passages(key, part):
    return joint_embeddings(key)[1]


def with_ends(entries, key, low, high):
    dims = entries.shape
    index_at = [jax.random.randint(jax.random.fold_in(key, axis), (), 0, dims[axis]) for axis in range(len(dims))]
    entries = entries.at[tuple(index_at)].set(low)
    longest = dims.index(max(dims))
    index_at[longest] = (index_at[longest] + 1) % dims[longest]
    return entries.at[tuple(index_at)].set(high)


def rank_bounds(count, slope):
    weights = [(1 << 20) // math.isqrt(grade ** slope) + 1 for grade in range(1, count + 1)]
    deviation = 1 + sum(weights) // (1 << 30)
    return np.cumsum(np.array([max(1, weight // deviation) for weight in weights]))


def ranked_ids(stream_key, dims, number_of, slope):
    table = rank_bounds(number_of, slope)
    ticket = jax.random.randint(jax.random.fold_in(stream_key, 1), dims, 0, int(table[number_of - 1]))
    rank = jnp.searchsorted(jnp.asarray(table, jnp.int32), ticket, side="right")
    return jax.random.permutation(jax.random.fold_in(stream_key, 2), number_of)[rank].astype(jnp.int32)


def setup_inputs(seed: int = 0) -> dict:
    streams_of = jax.random.split(jax.random.key(seed), 4)
    return {
        "queries": draw_queries(jax.random.fold_in(streams_of[3], 71), 0),
        "passages": draw_passages(jax.random.fold_in(streams_of[3], 71), 0),
        "hard_ids": with_ends(ranked_ids(streams_of[2], (NQ, HARD), NP, 2), jax.random.fold_in(streams_of[2], 3), 0, NP - 1).astype(jnp.int32),
    }


def reference(queries, passages, hard_ids):
    block = math.gcd(NQ, 512)
    nblocks = NQ // block
    scale = 1.0 / math.sqrt(D)
    column_ids = jnp.arange(NP, dtype=jnp.int32)

    def one_block(carry, index):
        loss_sum, passage_acc = carry
        begin = (index * block).astype(jnp.int32)
        query_rows = lax.dynamic_slice_in_dim(queries, begin, block, 0)
        id_rows = lax.dynamic_slice_in_dim(hard_ids, begin, block, 0)
        logits = jnp.dot(query_rows, passages.T, precision=lax.Precision.HIGHEST, preferred_element_type=jnp.float32) * scale
        counts = jnp.ones(logits.shape, jnp.float32)
        for k in range(HARD):
            counts = counts + (id_rows[:, k:k + 1] == column_ids[None, :]).astype(jnp.float32)
        row_max = lax.optimization_barrier(jnp.max(logits, axis=1))
        row_total = lax.optimization_barrier(jnp.sum(counts * jnp.exp(logits - row_max[:, None]), axis=1))
        lse = row_max + jnp.log(row_total)
        query_ids = begin + jnp.arange(block, dtype=jnp.int32)
        positive = column_ids[None, :] == query_ids[:, None]
        pos_logit = lax.optimization_barrier(jnp.sum(jnp.where(positive, logits, 0.0), axis=1))
        coeff = counts * jnp.exp(logits - lse[:, None]) - positive.astype(jnp.float32)
        query_part = jnp.dot(coeff, passages, precision=lax.Precision.HIGHEST, preferred_element_type=jnp.float32) * scale
        passage_acc = passage_acc + jnp.dot(coeff.T, query_rows, precision=lax.Precision.HIGHEST, preferred_element_type=jnp.float32) * scale
        return ((loss_sum + jnp.sum(lse - pos_logit), passage_acc), query_part)
    start_carry = (jnp.zeros((), jnp.float32), jnp.zeros((NP, D), jnp.float32))
    (loss_sum, passage_grads), query_parts = lax.scan(one_block, start_carry, jnp.arange(nblocks, dtype=jnp.int32))
    return (loss_sum / NQ, query_parts.reshape(NQ, D), passage_grads)
```

```python
import functools
import math

import jax
import jax.numpy as jnp
from jax import lax
from jax.experimental import pallas as pl
from jax.experimental.pallas import tpu as pltpu
from jax.sharding import PartitionSpec as P

HARD = 7
AXES = ("pb", "pa")
N_PB, N_PA = 16, 8
INTERPRET = False
F32, BF16 = jnp.float32, jnp.bfloat16
MIB = 1 << 20


def route(z=0, xl=0, core=0, y=0, xh=0, yxor=0, zxor=0):
    pairs = []
    for device in range(N_PB * N_PA):
        pb, pa = divmod(device, N_PA)
        to_z = ((pb // 4 + z) % 4) ^ zxor
        to_y = ((pa // 2 + y) % 4) ^ yxor
        to_pb = to_z * 4 + ((pb // 2 % 2) ^ xl) * 2 + (pb % 2 ^ core)
        pairs.append((device, to_pb * N_PA + to_y * 2 + (pa % 2 ^ xh)))
    return pairs


def send(x, **to):
    return lax.ppermute(x, AXES, route(**to))


def params(limit=40):
    return pltpu.CompilerParams(vmem_limit_bytes=limit * MIB)


def halves(x):
    hi = x.astype(BF16)
    return hi, (x - hi.astype(F32)).astype(BF16)


def split_kernel(a_ref, b_ref, hi_ref, lo_ref):
    own = pl.program_id(0) < pl.num_programs(0) // 2

    def put(ref):
        hi_ref[...], lo_ref[...] = halves(ref[...])

    pl.when(own)(lambda: put(a_ref))
    pl.when(jnp.logical_not(own))(lambda: put(b_ref))


def split_rows(a, b):
    rows, width = a.shape
    tile = min(256, rows)
    steps = rows // tile
    out = jax.ShapeDtypeStruct((2 * rows, width), BF16)
    return pl.pallas_call(
        split_kernel,
        out_shape=(out, out),
        grid=(2 * steps,),
        in_specs=[
            pl.BlockSpec((tile, width), lambda t: (jnp.minimum(t, steps - 1), 0)),
            pl.BlockSpec((tile, width), lambda t: (jnp.maximum(t - steps, 0), 0)),
        ],
        out_specs=[pl.BlockSpec((tile, width), lambda t: (t, 0))] * 2,
        compiler_params=params(),
        cost_estimate=pl.CostEstimate(flops=4 * rows * width, bytes_accessed=16 * rows * width, transcendentals=0),
        interpret=INTERPRET,
        name="split_rows",
    )(a, b)


NT = (((1,), (1,)), ((), ()))
TN = (((0,), (0,)), ((), ()))


def dot(a, b, dims):
    return lax.dot_general(a, b, dims, preferred_element_type=F32)


def score_kernel(rows, first, scale, base_ref, *refs):
    count = len(rows)
    blocks = refs[:count]
    qh_ref, ql_ref, ids_ref = refs[count : count + 3]
    refs = refs[count + 3 :]
    prev_ref = None
    if not first:
        prev_ref, refs = refs[0], refs[1:]
    e_ref, stat_ref, hi_ref, lo_ref, both = refs
    total = sum(rows)
    step = pl.program_id(0)
    tile = qh_ref.shape[0]

    @pl.when(step == 0)
    def _():
        at = 0
        for block, n in zip(blocks, rows):
            hi, lo = halves(block[...])
            both[at : at + n, :] = hi
            both[total + at : total + at + n, :] = lo
            hi_ref[at : at + n, :] = hi
            lo_ref[at : at + n, :] = lo
            at += n

    x = dot(both[...], qh_ref[...], NT)
    y = dot(both[:total, :], ql_ref[...], NT)
    s = (x[:total] + x[total:] + y) * scale
    top = jnp.max(s, axis=0, keepdims=True)
    if first:
        high = top
    else:
        before = prev_ref[0:1, :]
        high = jnp.maximum(before, top)
    e = jnp.exp(s - high)
    ids = ids_ref[...]
    parts = []
    at = 0
    for index, n in enumerate(rows):
        near = ids - base_ref[index]
        row = lax.broadcasted_iota(jnp.int32, (n, tile), 0)
        c = jnp.ones((n, tile), F32)
        for k in range(HARD):
            c = c + jnp.where(row == near[k : k + 1, :], 1.0, 0.0)
        parts.append(c * e[at : at + n])
        at += n
    ce = parts[0] if count == 1 else jnp.concatenate(parts, axis=0)
    mass = jnp.sum(ce, axis=0, keepdims=True)
    if first:
        lane = lax.broadcasted_iota(jnp.int32, (total, tile), 1) + step * tile - base_ref[count]
        positive = lax.broadcasted_iota(jnp.int32, (total, tile), 0) == lane
        pos = jnp.sum(jnp.where(positive, s, 0.0), axis=0, keepdims=True)
        ce = jnp.where(positive, 0.0, ce)
    else:
        pos = prev_ref[2:3, :]
        mass = mass + prev_ref[1:2, :] * jnp.exp(before - high)
    e_ref[...] = ce
    stat_ref[...] = jnp.concatenate([high, mass, pos, jnp.zeros((5, tile), F32)], axis=0)


def score(blocks, bases, qh, ql, ids, prev, scale):
    rows = tuple(b.shape[0] for b in blocks)
    total = sum(rows)
    queries, width = qh.shape
    tile = min(256, queries)
    whole = [pl.BlockSpec((n, width), lambda t, s: (0, 0)) for n in rows]
    args = list(blocks) + [qh, ql, ids]
    specs = whole + [
        pl.BlockSpec((tile, width), lambda t, s: (t, 0)),
        pl.BlockSpec((tile, width), lambda t, s: (t, 0)),
        pl.BlockSpec((8, tile), lambda t, s: (0, t)),
    ]
    if prev is not None:
        args.append(prev)
        specs.append(pl.BlockSpec((8, tile), lambda t, s: (0, t)))
    return pl.pallas_call(
        functools.partial(score_kernel, rows, prev is None, scale),
        out_shape=(
            jax.ShapeDtypeStruct((total, queries), F32),
            jax.ShapeDtypeStruct((8, queries), F32),
            jax.ShapeDtypeStruct((total, width), BF16),
            jax.ShapeDtypeStruct((total, width), BF16),
        ),
        grid_spec=pltpu.PrefetchScalarGridSpec(
            num_scalar_prefetch=1,
            grid=(queries // tile,),
            in_specs=specs,
            out_specs=[
                pl.BlockSpec((total, tile), lambda t, s: (0, t)),
                pl.BlockSpec((8, tile), lambda t, s: (0, t)),
                pl.BlockSpec((total, width), lambda t, s: (0, 0)),
                pl.BlockSpec((total, width), lambda t, s: (0, 0)),
            ],
            scratch_shapes=[pltpu.VMEM((2 * total, width), BF16)],
        ),
        compiler_params=params(),
        cost_estimate=pl.CostEstimate(
            flops=6 * total * queries * width, bytes_accessed=4 * (total * width + queries * width + total * queries), transcendentals=total * queries
        ),
        interpret=INTERPRET,
        name=f"score_{total}",
    )(bases, *args)


def query_kernel(groups, *refs):
    e_refs, stat_refs = refs[:groups], refs[groups : 2 * groups]
    hi_refs, lo_refs = refs[2 * groups : 3 * groups], refs[3 * groups : 4 * groups]
    out_ref = refs[4 * groups]
    last = stat_refs[-1][0:1, :]
    acc = None
    for g in range(groups):
        a = e_refs[g][...]
        if g < groups - 1:
            a = a * jnp.exp(stat_refs[g][0:1, :] - last)
        hi, lo = halves(a)
        ph, pw = hi_refs[g][...], lo_refs[g][...]
        part = dot(hi, ph, TN) + dot(lo, ph, TN) + dot(hi, pw, TN)
        acc = part if acc is None else acc + part
    out_ref[...] = acc


def query_part(es, stats, his, los, first_row, n_rows):
    width = his[0].shape[1]
    tile = min(256, n_rows)
    start = first_row // tile
    groups = len(es)
    depth = sum(e.shape[0] for e in es)
    specs = [pl.BlockSpec((e.shape[0], tile), lambda t: (0, t + start)) for e in es]
    specs += [pl.BlockSpec((8, tile), lambda t: (0, t + start))] * groups
    specs += [pl.BlockSpec(h.shape, lambda t: (0, 0)) for h in his] * 2
    return pl.pallas_call(
        functools.partial(query_kernel, groups),
        out_shape=jax.ShapeDtypeStruct((n_rows, width), F32),
        grid=(n_rows // tile,),
        in_specs=specs,
        out_specs=pl.BlockSpec((tile, width), lambda t: (t, 0)),
        compiler_params=params(),
        cost_estimate=pl.CostEstimate(
            flops=6 * depth * n_rows * width, bytes_accessed=4 * (depth * width + n_rows * width + depth * n_rows), transcendentals=0
        ),
        interpret=INTERPRET,
        name="query_part",
    )(*es, *stats, *his, *los)


def passage_kernel(rows, scale, e_ref, stat_ref, lse_ref, qh_ref, ql_ref, *refs):
    outs, both = refs[:-1], refs[-1]
    total = sum(rows)

    @pl.when(pl.program_id(0) == 0)
    def _():
        a = e_ref[...] * (jnp.exp(stat_ref[0:1, :] - lse_ref[0:1, :]) * scale)
        hi, lo = halves(a)
        both[:total, :] = hi
        both[total:, :] = lo

    x = jnp.dot(both[...], qh_ref[...], preferred_element_type=F32)
    y = jnp.dot(both[:total, :], ql_ref[...], preferred_element_type=F32)
    r = x[:total] + x[total:] + y
    at = 0
    for out, n in zip(outs, rows):
        out[...] = r[at : at + n]
        at += n


def passage_part(e, stat, lse, qh, ql, rows, scale):
    total, queries = e.shape
    width = qh.shape[1]
    tile = min(256, width)
    return pl.pallas_call(
        functools.partial(passage_kernel, tuple(rows), scale),
        out_shape=tuple(jax.ShapeDtypeStruct((n, width), F32) for n in rows),
        grid=(width // tile,),
        in_specs=[
            pl.BlockSpec((total, queries), lambda t: (0, 0)),
            pl.BlockSpec((8, queries), lambda t: (0, 0)),
            pl.BlockSpec((8, queries), lambda t: (0, 0)),
            pl.BlockSpec((queries, tile), lambda t: (0, t)),
            pl.BlockSpec((queries, tile), lambda t: (0, t)),
        ],
        out_specs=[pl.BlockSpec((n, tile), lambda t: (0, t)) for n in rows],
        scratch_shapes=[pltpu.VMEM((2 * total, queries), BF16)],
        compiler_params=params(),
        cost_estimate=pl.CostEstimate(
            flops=6 * total * queries * width, bytes_accessed=4 * (total * width + queries * width + total * queries), transcendentals=0
        ),
        interpret=INTERPRET,
        name=f"passage_part_{total}",
    )(e, stat, lse, qh, ql)


def merge(a, b):
    keep = a[0] >= b[0]
    small, big = jnp.where(keep, b[1], a[1]), jnp.where(keep, a[1], b[1])
    total = big + small * jnp.exp(-jnp.abs(a[0] - b[0]))
    return jnp.stack([jnp.maximum(a[0], b[0]), total, a[2] + b[2]])


def scatter_sum(blocks, plus, minus, swap):
    half = blocks[0][0].shape[0] // 2
    sums = []
    for dx in (1, 0):
        near, right, far, left = blocks[dx][0], blocks[dx][1], blocks[dx][2], blocks[dx][3]
        from_left = plus(far[:half])
        from_right = minus(far[half:])
        right = jnp.concatenate([right[:half] + from_left, right[half:]], axis=0)
        left = jnp.concatenate([left[:half], left[half:] + from_right], axis=0)
        near = near + plus(right) + minus(left)
        sums.append(swap(near) if dx == 1 else near)
    return sums[0] + sums[1]


def on_device(queries, passages, hard_ids):
    block, width = queries.shape
    shard = passages.shape[0]
    half = shard // 2
    scale = 1.0 / math.sqrt(width)
    pb, pa = lax.axis_index("pb"), lax.axis_index("pa")
    z, xl, core = pb // 4, pb // 2 % 2, pb % 2
    y, xh = pa // 2, pa % 2

    ids = jnp.concatenate([hard_ids.T, jnp.full((8 - HARD, block), -1, jnp.int32)], axis=0)
    across = send(passages, xl=1)
    down = send(passages, z=1)
    up = send(passages, z=-1)
    partner = send(queries, core=1)
    ids = jnp.concatenate([ids, send(ids, core=1)], axis=1)
    qh, ql = split_rows(queries, partner)

    def base(dz, dx, offset=0):
        owner = ((z + dz) % 4) * 4 + (xl ^ dx) * 2 + core
        return (owner * N_PA + pa) * shard + offset

    def bases(*entries):
        return jnp.stack(entries).astype(jnp.int32)

    groups = []
    prev = None

    def run(blocks, at):
        nonlocal prev
        e, prev, hi, lo = score(blocks, at, qh, ql, ids, prev, scale)
        groups.append((e, prev, hi, lo))

    run([passages], bases(base(0, 0), pa * shard))
    down_x = send(across, z=1)
    up_x = send(across, z=-1)
    far_a = send(down[:half], z=1)
    far_b = send(up[half:], z=-1)
    run([across, down, up], bases(base(0, 1), base(3, 0), base(1, 0)))
    far_xa = send(down_x[:half], z=1)
    far_xb = send(up_x[half:], z=-1)
    run([down_x, up_x, far_a, far_b], bases(base(3, 1), base(1, 1), base(2, 0), base(2, 0, half)))
    run([far_xa, far_xb], bases(base(2, 1), base(2, 1, half)))

    es, stats, his, los = (list(t) for t in zip(*groups))

    mine = prev[:3]
    other = send(mine, core=1)
    other = jnp.concatenate([other[:, block:], other[:, :block]], axis=1)
    rec = merge(mine, other)
    for to in (dict(yxor=1), dict(yxor=2), dict(xh=1)):
        rec = merge(rec, send(rec, **to))

    quarter = block // 2
    theirs = [query_part(es, stats, his, los, block + r, quarter) for r in (0, quarter)]
    ours = [query_part(es, stats, his, los, r, quarter) for r in (0, quarter)]
    from_partner = [send(t, core=1) for t in theirs]

    lse = rec[0] + jnp.log(rec[1])
    lse8 = jnp.broadcast_to(lse[None, :], (8, 2 * block))

    (g21,) = passage_part(es[3], stats[3], lse8, qh, ql, (shard,), scale)
    g31, g11, g20 = passage_part(es[2], stats[2], lse8, qh, ql, (shard,) * 3, scale)
    g01, g30, g10 = passage_part(es[1], stats[1], lse8, qh, ql, (shard,) * 3, scale)
    (g00,) = passage_part(es[0], stats[0], lse8, qh, ql, (shard,), scale)
    passage_sum = scatter_sum(
        [[g00, g10, g20, g30], [g01, g11, g21, g31]],
        lambda v: send(v, z=1),
        lambda v: send(v, z=-1),
        lambda v: send(v, xl=1),
    )

    ours, from_partner = jnp.concatenate(ours, 0), jnp.concatenate(from_partner, 0)
    own_scale = (jnp.exp(mine[0, :block] - lse[:block]) * scale)[:, None]
    other_scale = (jnp.exp(other[0, :block] - lse[:block]) * scale)[:, None]

    def rows_for(dy, dx):
        at = (((y + dy) % 4) * 2 + (xh ^ dx)) * shard

        def cut(v):
            return lax.dynamic_slice_in_dim(v, at, shard, 0)

        return cut(ours) * cut(own_scale) + cut(from_partner) * cut(other_scale)

    query_sum = scatter_sum(
        [[rows_for(dy, dx) for dy in range(4)] for dx in range(2)],
        lambda v: send(v, y=1),
        lambda v: send(v, y=-1),
        lambda v: send(v, xh=1),
    )

    def own(v):
        return lax.dynamic_slice_in_dim(v, pa * shard, shard, 0)

    row_ids = pb * block + pa * shard + jnp.arange(shard, dtype=jnp.int32)
    own_ids = lax.dynamic_slice_in_dim(ids, pa * shard, shard, 1)
    tally = 1.0 + jnp.sum((own_ids == row_ids[None, :]).astype(F32), axis=0)
    coeff = (tally * jnp.exp(own(rec[2]) - own(lse)) - 1.0) * scale
    query_grads = query_sum + coeff[:, None] * passages
    passage_grads = passage_sum + coeff[:, None] * own(queries)

    sums = jnp.sum((lse - rec[2]).reshape(2, block), axis=1)
    loss = jnp.broadcast_to(sums[0] + sums[1], (8, 128))
    for to in (dict(zxor=1), dict(zxor=2), dict(xl=1)):
        loss = loss + send(loss, **to)
    loss = loss[0, 0] / (block * N_PB)
    return loss, query_grads, passage_grads


def solution(mesh):
    placed = (P("pb", None), P(("pb", "pa"), None), P("pb", None))
    return jax.shard_map(
        on_device,
        mesh=mesh,
        in_specs=placed,
        out_specs=(P(), P(("pb", "pa"), None), P(("pb", "pa"), None)),
        check_vma=False,
    )
```
